32 devices in a mesh: dp: 4 (over x, core), fsdp: 2 (over y), enc: 4 (over z).
Axes of the slice: x: 2, y: 2, z: 4, core: 2. Of those that a mesh axis runs over, the one named last changes fastest.
Arguments:
- hidden: bfloat16 [8192, 8192], P(('dp', 'fsdp', 'enc')), may hold values from -40 to 40
- residual_gradient: bfloat16 [8192, 8192], P(('dp', 'fsdp', 'enc')), may hold values from -3 to 3
- value_output_gradient: bfloat16 [8192, 1024], P(('dp', 'fsdp', 'enc')), may hold values from -6 to 6
- attention_norm_gain: float32 [8192], replicated, may hold values from 0.1 to 1.9
- value_frozen_weight: bfloat16 [8192, 1024], P('fsdp'), may hold values from -0.0625 to 0.0625
- value_down_factor: bfloat16 [8192, 16], replicated, may hold values from -0.0625 to 0.0625
- value_up_factor: bfloat16 [16, 1024], replicated, may hold values from -0.29882812 to 0.29882812
- merger_frozen_weight: bfloat16 [5120, 8192], P(None, ('fsdp', 'enc')), may hold values from -0.078125 to 0.078125
- merger_down_factor: bfloat16 [5120, 16], replicated, may hold values from -0.078125 to 0.078125
- merger_up_factor: bfloat16 [16, 8192], P(None, ('fsdp', 'enc')), may hold values from -0.29882812 to 0.29882812
- merger_saved_preactivation: bfloat16 [1024, 5120], P(('dp', 'fsdp', 'enc')), may hold values from -5 to 5
- image_token_counts: int32 [32], P('dp'), may hold values from 8 to 16, as said below
- image_encoder_owner: int32 [32], P('dp'), may hold values from 0 to 7, as said below
- image_first_rows: int32 [32], P(('dp', 'fsdp', 'enc')), may hold values from 0 to 255, as said below
Outputs:
- layer_input_gradient: bfloat16 [8192, 8192], P(('dp', 'fsdp', 'enc'))
- preactivation_gradient: bfloat16 [1024, 5120], P(('dp', 'fsdp', 'enc'))
- value_down_gradient: float32 [8192, 16], replicated
- value_up_gradient: float32 [16, 1024], replicated
- merger_down_gradient: float32 [5120, 16], replicated
- merger_up_gradient: float32 [16, 8192], P(None, ('fsdp', 'enc'))
The draws below stay inside these ranges and needn't reach their ends.
Inputs may be any that keep to these rules, and one draw needn't show every extreme that they name: `image_token_counts`: within each data replica some encoder device owns exactly 2 images, all of 16 visual tokens, so its rows fill all 32; no other device owns more than 2 images. `image_encoder_owner`: encoder devices are numbered within the data replica in mesh order. `image_first_rows`: images of one device lie inside its 256 rows in increasing order and don't intersect.
All inputs are finite; a program needn't handle non-finite values.
Results may differ from the reference program's by a relative error of at most 0.0085.
Values may be sent and summed in bfloat16 or wider, within the bound.
No kernel may reach another device: no remote copies, remote signals or barrier semaphores. Data moves between devices by JAX's collectives and lax.ppermute only.
A program may use at most 192 MiB of HBM per device.

```python
import jax
import jax.numpy as jnp
from jax import lax

MODEL_WIDTH = 8192
VALUE_WIDTH = 1024
MERGE = 5120
ADAPTER_RANK = 16
TOK_DEV = 256
IMG_DEV = 1
MAXIMG = 16
OWNERS = 8
OCAP = 32
TOKENS = 8192
OWN_ROWS = 1024
N_DP = 4
N_FSDP = 2
N_ENC = 4


def image_layout(key):
    group_keys = jax.random.split(jax.random.fold_in(key, 11), N_DP)

    def one_group(group_key):
        subkeys = jax.random.split(group_key, 5)
        per_group = OWNERS * IMG_DEV
        busiest_load = 2 * IMG_DEV
        busiest = jax.random.randint(subkeys[0], (), 0, OWNERS)
        others = (busiest + 1 + jnp.arange((OWNERS - 1) * busiest_load) // busiest_load) % OWNERS
        others = jax.random.permutation(subkeys[1], others)[:per_group - busiest_load]
        listed = jnp.concatenate([jnp.zeros((busiest_load,), jnp.int32) + busiest, others.astype(jnp.int32)])
        listed = jax.random.permutation(subkeys[2], listed).astype(jnp.int32)
        counts = jax.random.randint(subkeys[3], (per_group,), MAXIMG // 2, MAXIMG + 1)
        counts = jnp.where(listed == busiest, MAXIMG, counts).astype(jnp.int32)
        spare_rows = (TOK_DEV - IMG_DEV * MAXIMG) // IMG_DEV
        text_gaps = jax.random.randint(subkeys[4], (OWNERS, IMG_DEV), 0, spare_rows + 1)
        shaped = counts.reshape(OWNERS, IMG_DEV)
        offsets = jnp.cumsum(text_gaps + shaped, axis=1) - shaped
        return (counts, listed, offsets.reshape(-1).astype(jnp.int32))
    counts, listed, offsets = jax.vmap(one_group)(group_keys)
    return (counts.reshape(-1).astype(jnp.int32), listed.reshape(-1).astype(jnp.int32), offsets.reshape(-1).astype(jnp.int32))


def draw_image_token_counts(key, part):
    return image_layout(key)[0]


def draw_image_encoder_owner(key, part):
    return image_layout(key)[1]


def draw_image_first_rows(key, part):
    return image_layout(key)[2]


def draw_hidden(key, part):
    subkeys = jax.random.split(jax.random.fold_in(key, 3), 3)
    values = jax.random.normal(subkeys[0], (TOKENS, MODEL_WIDTH), jnp.float32)
    row_scale = jnp.exp(jax.random.uniform(subkeys[1], (TOKENS, 1), jnp.float32, -1.2, 1.2))
    column_scale = jnp.exp(jax.random.uniform(subkeys[2], (1, MODEL_WIDTH), jnp.float32, -1.2, 1.2))
    return jnp.clip(values * row_scale * column_scale, -40.0, 40.0).astype(jnp.bfloat16)


def levels(rng, extent, shards, low, largest):
    level = 1.0
    for axis_at, parts in shards:
        steps = jax.random.uniform(jax.random.fold_in(jax.random.fold_in(rng, 6), axis_at), (parts,), jnp.float32, low / len(shards), largest / len(shards))
        level = level * jnp.repeat(jnp.exp(steps), extent[axis_at] // parts).reshape((-1,) + (1,) * (len(extent) - 1 - axis_at))
    return level


def gaussian(rng, shape, width, reach, shards=(), held_as=jnp.bfloat16):
    level = levels(rng, shape, shards, -0.22, 0.18) if shards else 1.0
    values = jax.random.normal(rng, shape, jnp.float32) * width * level
    return jnp.minimum(jnp.maximum(values, -reach), reach).astype(held_as)


def setup_inputs(seed: int = 0) -> dict:
    key_of = jax.random.split(jax.random.key(seed), 15)
    hidden = draw_hidden(jax.random.fold_in(key_of[14], 71), 0)
    residual_gradient = gaussian(key_of[1], (TOKENS, MODEL_WIDTH), 0.5, 3.0, ((0, 32),))
    value_output_gradient = gaussian(key_of[2], (TOKENS, VALUE_WIDTH), 1.0, 6.0, ((0, 32),))
    attention_norm_gain = jnp.clip(1.0 + 0.18 * jax.random.normal(key_of[3], (MODEL_WIDTH,), jnp.float32), 0.1, 1.9)
    value_frozen_weight = gaussian(key_of[4], (MODEL_WIDTH, VALUE_WIDTH), MODEL_WIDTH ** -0.5, 0.0625, ((0, 2),))
    value_down_factor = gaussian(key_of[5], (MODEL_WIDTH, ADAPTER_RANK), MODEL_WIDTH ** -0.5, 0.0625)
    value_up_factor = gaussian(key_of[6], (ADAPTER_RANK, VALUE_WIDTH), 0.05, 0.29882812)
    merger_frozen_weight = gaussian(key_of[7], (MERGE, MODEL_WIDTH), MERGE ** -0.5, 0.078125, ((1, 8),))
    merger_down_factor = gaussian(key_of[8], (MERGE, ADAPTER_RANK), MERGE ** -0.5, 0.078125)
    merger_up_factor = gaussian(key_of[9], (ADAPTER_RANK, MODEL_WIDTH), 0.05, 0.29882812, ((1, 8),))
    merger_saved_preactivation = gaussian(key_of[10], (OWN_ROWS, MERGE), 1.0, 5.0, ((0, 32),))
    image_token_counts = draw_image_token_counts(jax.random.fold_in(key_of[14], 71), 0)
    image_encoder_owner = draw_image_encoder_owner(jax.random.fold_in(key_of[14], 71), 0)
    image_first_rows = draw_image_first_rows(jax.random.fold_in(key_of[14], 71), 0)
    return dict(hidden=hidden, residual_gradient=residual_gradient, value_output_gradient=value_output_gradient, attention_norm_gain=attention_norm_gain, value_frozen_weight=value_frozen_weight, value_down_factor=value_down_factor, value_up_factor=value_up_factor, merger_frozen_weight=merger_frozen_weight, merger_down_factor=merger_down_factor, merger_up_factor=merger_up_factor, merger_saved_preactivation=merger_saved_preactivation, image_token_counts=image_token_counts, image_encoder_owner=image_encoder_owner, image_first_rows=image_first_rows)


adapter_scale = 2.0
norm_eps = 1e-06

def gelu_parts(preact):
    normal_cdf = 0.5 * (1.0 + lax.erf(preact * 0.7071067811865476))
    normal_pdf = jnp.exp(-0.5 * preact * preact) * 0.3989422804014327
    return (normal_cdf, normal_pdf)

def owner_layout(image_token_counts, image_encoder_owner, owner_count, owner_room, slot_len):
    total_images = image_token_counts.shape[0]
    image_ids = jnp.arange(total_images).astype(jnp.int32)
    same_owner = image_encoder_owner[:, None] == image_encoder_owner[None, :]
    earlier = image_ids[None, :] < image_ids[:, None]
    starts = lax.optimization_barrier(jnp.sum(jnp.where(same_owner & earlier, image_token_counts[None, :], 0), axis=1)).astype(jnp.int32)
    row_index = jnp.arange(owner_count * owner_room).astype(jnp.int32)
    row_owner = (row_index // owner_room).astype(jnp.int32)
    row_place = (row_index % owner_room).astype(jnp.int32)
    matches = (row_owner[:, None] == image_encoder_owner[None, :]) & (row_place[:, None] >= starts[None, :]) & (row_place[:, None] < (starts + image_token_counts)[None, :])
    source = lax.optimization_barrier(jnp.sum(jnp.where(matches, image_ids[None, :] * slot_len + row_place[:, None] - starts[None, :], 0), axis=1)).astype(jnp.int32)
    valid_rows = jnp.any(matches, axis=1)
    return (source, valid_rows)

def take_slots(layer_input_gradient, counts_in, offsets_in):
    padded = jnp.concatenate([layer_input_gradient, jnp.zeros((MAXIMG, layer_input_gradient.shape[1]), layer_input_gradient.dtype)], axis=0)
    pieces = []
    for image_index in range(offsets_in.shape[0]):
        window = lax.dynamic_slice_in_dim(padded, offsets_in[image_index], MAXIMG, 0)
        inside = jnp.arange(MAXIMG) < counts_in[image_index]
        pieces.append(jnp.where(inside[:, None], window, jnp.zeros_like(window)))
    return jnp.concatenate(pieces, axis=0)

def decoder_layer_block(incoming_rows, residual_input, value_incoming, attention_norm_gain, passed_gradient, value_down_factor, value_up_factor):
    values = incoming_rows.astype(jnp.float32)
    inverse = lax.rsqrt(lax.optimization_barrier(jnp.mean(values * values, axis=1, keepdims=True)) + norm_eps)
    gain_values = attention_norm_gain.astype(jnp.float32)
    normalized_input = (values * inverse * gain_values).astype(jnp.bfloat16)
    value_low_product = jnp.dot(value_incoming, value_up_factor.T, preferred_element_type=jnp.float32).astype(jnp.bfloat16)
    normalized_gradient = passed_gradient.astype(jnp.float32) + adapter_scale * jnp.dot(value_low_product, value_down_factor.T, preferred_element_type=jnp.float32)
    gained = gain_values * normalized_gradient
    layer_input_gradient = (residual_input.astype(jnp.float32) + inverse * gained - values * inverse ** 3 * lax.optimization_barrier(jnp.mean(values * gained, axis=1, keepdims=True))).astype(jnp.bfloat16)
    projected_rows = jnp.dot(normalized_input, value_down_factor, preferred_element_type=jnp.float32).astype(jnp.bfloat16)
    up_term = lax.dot_general(projected_rows, value_incoming, (((0,), (0,)), ((), ())), preferred_element_type=jnp.float32)
    down_term = lax.dot_general(normalized_input, value_low_product, (((0,), (0,)), ((), ())), preferred_element_type=jnp.float32)
    return (layer_input_gradient, down_term, up_term)

def reference(hidden, residual_gradient, value_output_gradient, attention_norm_gain, value_frozen_weight, value_down_factor, value_up_factor, merger_frozen_weight, merger_down_factor, merger_up_factor, merger_saved_preactivation, image_token_counts, image_encoder_owner, image_first_rows):
    device_total = N_DP * N_FSDP * N_ENC
    owner_count = N_FSDP * N_ENC
    gradient_scale = 256.0 / TOKENS
    value_transposed = value_frozen_weight.T

    def device_step(running, inputs):
        incoming_rows, residual_input, value_incoming, counts_in, offsets_in = inputs
        passed_gradient = jnp.dot(value_incoming, value_transposed, preferred_element_type=jnp.float32).astype(jnp.bfloat16)
        layer_input_gradient, down_term, up_term = decoder_layer_block(incoming_rows, residual_input, value_incoming, attention_norm_gain, passed_gradient, value_down_factor, value_up_factor)
        slots_out = take_slots(layer_input_gradient, counts_in, offsets_in)
        return ((running[0] + down_term, running[1] + up_term), (layer_input_gradient, slots_out))
    start_sums = (jnp.zeros((MODEL_WIDTH, ADAPTER_RANK), jnp.float32), jnp.zeros((ADAPTER_RANK, VALUE_WIDTH), jnp.float32))
    scanned = (hidden.reshape(device_total, TOK_DEV, MODEL_WIDTH), residual_gradient.reshape(device_total, TOK_DEV, MODEL_WIDTH), value_output_gradient.reshape(device_total, TOK_DEV, VALUE_WIDTH), image_token_counts.reshape(device_total, IMG_DEV), image_first_rows.reshape(device_total, IMG_DEV))
    sums, outputs = lax.scan(device_step, start_sums, scanned)
    layer_input_gradient = outputs[0].reshape(TOKENS, MODEL_WIDTH)
    group_slots = outputs[1].reshape(N_DP, owner_count * IMG_DEV * MAXIMG, MODEL_WIDTH)
    merger_weight_transposed = merger_frozen_weight.T
    merger_b_transposed = merger_up_factor.T
    merger_down_widened = merger_down_factor.astype(jnp.float32).T

    def group_step(inputs):
        slots_in, counts_in, owners_in, preact_in = inputs
        source, valid_rows = owner_layout(counts_in, owners_in, owner_count, OCAP, MAXIMG)
        visual_tokens = jnp.where(valid_rows[:, None], jnp.take(slots_in, source, axis=0), jnp.zeros((), slots_in.dtype))
        merger_low_product = jnp.dot(visual_tokens, merger_b_transposed, preferred_element_type=jnp.float32)
        combined_gradient = jnp.dot(visual_tokens, merger_weight_transposed, preferred_element_type=jnp.float32) + adapter_scale * jnp.dot(merger_low_product, merger_down_widened, precision=lax.Precision.HIGHEST)
        preact = preact_in.astype(jnp.float32)
        normal_cdf, normal_pdf = gelu_parts(preact)
        preactivation_gradient = (combined_gradient * (normal_cdf + preact * normal_pdf)).astype(jnp.bfloat16)
        activation = (preact * normal_cdf).astype(jnp.bfloat16)
        act_low = jnp.dot(activation, merger_down_factor, preferred_element_type=jnp.float32).astype(jnp.bfloat16)
        term_b2 = lax.dot_general(act_low, visual_tokens, (((0,), (0,)), ((), ())), preferred_element_type=jnp.float32)
        term_a2 = lax.dot_general(activation, merger_low_product.astype(jnp.bfloat16), (((0,), (0,)), ((), ())), preferred_element_type=jnp.float32)
        return (preactivation_gradient, term_b2, term_a2)
    grouped = (group_slots, image_token_counts.reshape(N_DP, -1), image_encoder_owner.reshape(N_DP, -1), merger_saved_preactivation.reshape(N_DP, owner_count * OCAP, MERGE))
    pre_grads, terms_b2, terms_a2 = lax.map(group_step, grouped)
    scale_factor = gradient_scale * adapter_scale
    return (layer_input_gradient, pre_grads.reshape(OWN_ROWS, MERGE), scale_factor * sums[0], scale_factor * sums[1], scale_factor * lax.optimization_barrier(jnp.sum(terms_a2, axis=0)), scale_factor * lax.optimization_barrier(jnp.sum(terms_b2, axis=0)))
```

```python
import jax
import jax.numpy as jnp
from jax import lax
from jax.sharding import PartitionSpec as P

MAXIMG = 16
LANES = 128

adapter_scale = 2.0
norm_eps = 1e-06

bf16 = jnp.bfloat16
f32 = jnp.float32


def gelu_parts(preact):
    normal_cdf = 0.5 * (1.0 + lax.erf(preact * 0.7071067811865476))
    normal_pdf = jnp.exp(-0.5 * preact * preact) * 0.3989422804014327
    return (normal_cdf, normal_pdf)


def nt(a, b, **kw):
    return lax.dot_general(a, b, (((1,), (1,)), ((), ())), preferred_element_type=f32, **kw)


def tn(a, b, **kw):
    return lax.dot_general(a, b, (((0,), (0,)), ((), ())), preferred_element_type=f32, **kw)


def swap(x, axis, k):
    size = lax.axis_size(axis)
    return lax.ppermute(x, axis, [(q, q ^ k) for q in range(size)])


def bits_of(axes):
    return [(axis, 1 << b) for axis in axes for b in range(lax.axis_size(axis).bit_length() - 1)]


def bit_at(axis, k):
    return (lax.axis_index(axis) // k) % 2


def split_dim(shape):
    return 1 if shape[1] % (2 * LANES) == 0 else 0


def half(x, dim, which):
    size = x.shape[dim] // 2
    return lax.dynamic_slice_in_dim(x, which * size, size, dim)


def all_sum(groups):
    arrays = [a for a, _ in groups]
    steps = [bits_of(axes) for _, axes in groups]
    longest = max(steps, key=len)
    dims = [[] for _ in groups]
    for at, (axis, k) in enumerate(longest):
        bit = bit_at(axis, k)
        sent, kept, users = [], [], []
        for g, s in enumerate(steps):
            if at < len(s):
                d = split_dim(arrays[g].shape)
                dims[g].append(d)
                kept.append(half(arrays[g], d, bit))
                sent.append(half(arrays[g], d, 1 - bit).astype(bf16))
                users.append(g)
        got = swap_many(sent, axis, k)
        for g, a, r in zip(users, kept, got):
            arrays[g] = a + r.astype(f32)
    arrays = [a.astype(bf16) for a in arrays]
    for at, (axis, k) in reversed(list(enumerate(longest))):
        bit = bit_at(axis, k)
        users = [g for g, s in enumerate(steps) if at < len(s)]
        got = swap_many([arrays[g] for g in users], axis, k)
        for g, r in zip(users, got):
            d = dims[g][at]
            a = arrays[g]
            arrays[g] = jnp.concatenate(
                [jnp.where(bit == 0, a, r), jnp.where(bit == 0, r, a)], axis=d
            )
    return arrays


def swap_many(parts, axis, k):
    if len(parts) == 1:
        return [swap(parts[0], axis, k)]
    rows = max(p.shape[0] for p in parts)
    if all(p.shape[0] == rows for p in parts):
        got = swap(jnp.concatenate(parts, axis=1), axis, k)
        out, at = [], 0
        for p in parts:
            out.append(got[:, at : at + p.shape[1]])
            at += p.shape[1]
        return out
    return [swap(p, axis, k) for p in parts]


def passed_parts(rows, weight):
    size = lax.axis_size("fsdp")
    there = [swap(rows, "fsdp", k) for k in range(1, size)]
    sent = [nt(r, weight).astype(bf16) for r in there]
    back = [swap(c, "fsdp", k) for k, c in zip(range(1, size), sent)]
    return [nt(rows, weight).astype(bf16)] + back


def in_order(parts):
    size = len(parts)
    me = lax.axis_index("fsdp")
    k = 1
    while k < size:
        bit = (me // k) % 2
        step = list(parts)
        for i in range(size):
            step[i] = jnp.where(bit == 0, parts[i], parts[i ^ k])
        parts = step
        k *= 2
    return jnp.concatenate(parts, axis=1)


def layer_rows(values, residual, passed, lowrank, inverse, gain, down):
    normed_grad = passed.astype(f32) + adapter_scale * nt(lowrank, down)
    gained = gain * normed_grad
    return (
        residual.astype(f32)
        + inverse * gained
        - values * inverse**3 * jnp.mean(values * gained, axis=1, keepdims=True)
    ).astype(bf16)


def body(
    hidden,
    residual_gradient,
    value_output_gradient,
    attention_norm_gain,
    value_frozen_weight,
    value_down_factor,
    value_up_factor,
    merger_frozen_weight,
    merger_down_factor,
    merger_up_factor,
    merger_saved_preactivation,
    image_token_counts,
    image_encoder_owner,
    image_first_rows,
):
    model = ("fsdp", "enc")
    device_total = lax.axis_size("dp") * lax.axis_size("fsdp") * lax.axis_size("enc")
    scale_factor = (256.0 / (hidden.shape[0] * device_total)) * adapter_scale
    owners = lax.axis_size("fsdp") * lax.axis_size("enc")
    room, merge = merger_saved_preactivation.shape
    width = hidden.shape[1]
    rank = value_down_factor.shape[1]
    member = lax.axis_index(model)
    local_images = image_first_rows.shape[0]
    images = image_token_counts.shape[0]
    slots = images * MAXIMG
    gain = attention_norm_gain

    local_counts = lax.dynamic_slice_in_dim(
        image_token_counts, member * local_images, local_images, 0
    )

    def windows(x):
        return jnp.concatenate(
            [
                lax.dynamic_slice_in_dim(x, image_first_rows[i], MAXIMG, 0)
                for i in range(local_images)
            ],
            axis=0,
        )

    v_win = windows(value_output_gradient)
    passed_win = in_order(passed_parts(v_win, value_frozen_weight))
    x_win = windows(hidden).astype(f32)
    inv_win = lax.rsqrt(jnp.mean(x_win * x_win, axis=1, keepdims=True) + norm_eps)
    low_win = nt(v_win, value_up_factor).astype(bf16)
    lig_win = layer_rows(
        x_win, windows(residual_gradient), passed_win, low_win, inv_win, gain, value_down_factor
    )
    picks = []
    row = jnp.arange(MAXIMG)
    last = hidden.shape[0] - MAXIMG
    for i in range(local_images):
        shift = image_first_rows[i] - jnp.minimum(image_first_rows[i], last)
        picks.append(
            (row[None, :] == row[:, None] + shift) & (row[:, None] < local_counts[i])
        )
    slot_rows = jnp.concatenate(
        [
            jnp.dot(
                p.astype(bf16),
                lig_win[i * MAXIMG : (i + 1) * MAXIMG],
                preferred_element_type=f32,
            ).astype(bf16)
            for i, p in enumerate(picks)
        ],
        axis=0,
    )

    preact = merger_saved_preactivation.astype(f32)
    normal_cdf, normal_pdf = gelu_parts(preact)
    activation = (preact * normal_cdf).astype(bf16)
    act_low = jnp.dot(activation, merger_down_factor, preferred_element_type=f32).astype(bf16)

    block = width // owners
    local_slots = local_images * MAXIMG
    cut = slot_rows.reshape(local_slots, owners, block).transpose(1, 0, 2)
    extra = room * rank // local_slots
    side = jnp.broadcast_to(act_low.reshape(1, local_slots, extra), (owners, local_slots, extra))
    got = lax.all_to_all(
        jnp.concatenate([cut, side], axis=2), model, split_axis=0, concat_axis=0, tiled=True
    )
    visual = got[:, :, :block].reshape(slots, block)
    all_low = got[:, :, block:].reshape(owners * room, rank)

    ids = jnp.arange(images)
    same = image_encoder_owner[:, None] == image_encoder_owner[None, :]
    starts = jnp.sum(jnp.where(same & (ids[None, :] < ids[:, None]), image_token_counts[None, :], 0), axis=1)
    first = image_encoder_owner * room + starts
    dest = jnp.where(
        row[None, :] < image_token_counts[:, None], first[:, None] + row[None, :], -1
    ).reshape(slots)
    place = (jnp.arange(owners * room)[:, None] == dest[None, :]).astype(bf16)
    own_place = (member * room + jnp.arange(room)[:, None] == dest[None, :]).astype(f32)

    partial = lax.dot_general(
        visual,
        merger_frozen_weight.reshape(owners, merge // owners, block),
        (((1,), (2,)), ((), ())),
        preferred_element_type=f32,
    ).astype(bf16).transpose(1, 0, 2)
    low_part = nt(visual, merger_up_factor)
    summed = jnp.sum(
        lax.all_to_all(partial, model, split_axis=0, concat_axis=0, tiled=True).astype(f32), axis=0
    ).astype(bf16)
    routed = jnp.dot(place, summed, preferred_element_type=f32).astype(bf16)
    routed = lax.all_to_all(
        routed.reshape(owners, room, merge // owners), model, split_axis=0, concat_axis=0, tiled=True
    )
    merged = routed.transpose(1, 0, 2).reshape(room, merge).astype(f32)

    low_sum = low_part
    for axis, k in bits_of(model):
        low_sum = low_sum + swap(low_sum, axis, k)
    low_own = jnp.dot(own_place, low_sum, precision=lax.Precision.HIGHEST)
    merged = merged + adapter_scale * nt(
        low_own, merger_down_factor.astype(f32), precision=lax.Precision.HIGHEST
    )
    preactivation_gradient = (merged * (normal_cdf + preact * normal_pdf)).astype(bf16)

    values = hidden.astype(f32)
    inverse = lax.rsqrt(jnp.mean(values * values, axis=1, keepdims=True) + norm_eps)
    normed = (values * inverse * gain).astype(bf16)
    lowrank = nt(value_output_gradient, value_up_factor).astype(bf16)
    projected = jnp.dot(normed, value_down_factor, preferred_element_type=f32).astype(bf16)
    up_term = scale_factor * tn(projected, value_output_gradient)
    down_term = scale_factor * tn(lowrank, normed)
    merger_down_term = scale_factor * tn(low_own.astype(bf16), activation)
    slot_low = tn(place, all_low).astype(bf16)
    merger_up_term = scale_factor * tn(slot_low, visual)
    total, merger_up = all_sum(
        [
            (
                jnp.concatenate([down_term, up_term, merger_down_term], axis=1),
                ("dp",) + model,
            ),
            (merger_up_term, ("dp",)),
        ]
    )
    total = total.astype(f32)
    value_width = value_output_gradient.shape[1]
    value_down_gradient = total[:, :width].T
    value_up_gradient = total[:, width : width + value_width]
    merger_down_gradient = total[:, width + value_width :].T
    merger_up_gradient = merger_up.astype(f32)

    passed = in_order(passed_parts(value_output_gradient, value_frozen_weight))
    layer_input_gradient = layer_rows(
        values, residual_gradient, passed, lowrank, inverse, gain, value_down_factor
    )
    return (
        layer_input_gradient,
        preactivation_gradient,
        value_down_gradient,
        value_up_gradient,
        merger_down_gradient,
        merger_up_gradient,
    )


def solution(mesh):
    placed = (
        P(("dp", "fsdp", "enc"), None),
        P(("dp", "fsdp", "enc"), None),
        P(("dp", "fsdp", "enc"), None),
        P(),
        P("fsdp", None),
        P(),
        P(),
        P(None, ("fsdp", "enc")),
        P(),
        P(None, ("fsdp", "enc")),
        P(("dp", "fsdp", "enc"), None),
        P("dp"),
        P("dp"),
        P(("dp", "fsdp", "enc")),
    )
    return jax.shard_map(
        body,
        mesh=mesh,
        in_specs=placed,
        out_specs=(
            P(("dp", "fsdp", "enc"), None),
            P(("dp", "fsdp", "enc"), None),
            P(),
            P(),
            P(),
            P(None, ("fsdp", "enc")),
        ),
        check_vma=False,
    )
```
